512 devices in a mesh: ctx: 32 (over y, z_hi, core), ch: 16 (over z_lo, x).
Axes of the slice: x: 4, y: 8, z: 8 (z_hi: 2, z_lo: 4; z = z_hi * 4 + z_lo), core: 2. Of those that a mesh axis runs over, the one named last changes fastest.
Arguments:
- query_proj: bfloat16 [16384, 4096], P('ctx', 'ch'), may hold values from -6 to 6
- key_proj: bfloat16 [16384, 4096], P('ctx', 'ch'), may hold values from -6 to 6
- value_proj: bfloat16 [16384, 4096], P('ctx', 'ch'), may hold values from -6 to 6
- out_grad: bfloat16 [16384, 4096], P('ctx', 'ch'), may hold values from -6 to 6
- long_filter: bfloat16 [4096, 16384], P(None, ('ch', 'ctx')), as said below
- skip_gain: float32 [4096], P('ch'), may hold values from -4 to 4
Outputs:
- output: bfloat16 [16384, 4096], P('ctx', 'ch')
- query_grad: bfloat16 [16384, 4096], P('ctx', 'ch')
- key_grad: bfloat16 [16384, 4096], P('ctx', 'ch')
- value_grad: bfloat16 [16384, 4096], P('ctx', 'ch')
The draws below stay inside these ranges and needn't reach their ends.
Inputs may be any that keep to these rules, and one draw needn't show every extreme that they name: `long_filter`: each channel's filter is a rough sequence of taps under an envelope that falls with the tap index.
All inputs are finite; a program needn't handle non-finite values.
Results may differ from the reference program's by a relative error of at most 0.007.
Values may be sent and summed in bfloat16 or wider, within the bound.
A program may use at most 64 MiB of HBM per device.

```python
import math
import jax
import jax.numpy as jnp
from jax import lax

C = 4096
L = 16384


def draw_long_filter(key, part):
    keys = jax.random.split(key, 5)
    tap_index = jnp.arange(L, dtype=jnp.int32)[None, :]
    tap_float = tap_index.astype(jnp.float32)
    rough = jax.random.normal(keys[0], (C, L), jnp.float32)
    reach = jnp.exp(jax.random.uniform(keys[1], (C, 1), jnp.float32, math.log(20.0), math.log(4.0 * L)))
    envelope = jnp.exp(-tap_float / reach)
    spots = jax.random.randint(keys[2], (C, 3), 0, L)
    drops = jax.random.uniform(keys[3], (C, 3), jnp.float32, 0.5, 0.8)
    for index in range(3):
        envelope = envelope * jnp.where(tap_index >= spots[:, index:index + 1], drops[:, index:index + 1], 1.0)
    floor_level = jax.random.uniform(keys[4], (C, 1), jnp.float32, 0.4, 0.7)
    envelope = envelope + floor_level * jnp.exp(-tap_float / (2.0 * L))
    scale = jnp.sqrt(jnp.sum(envelope * envelope, axis=1, keepdims=True))
    return (rough * envelope / scale).astype(jnp.bfloat16)


def block_levels(key, shape, cuts, smallest, high):
    loudness, own = 1.0, jax.random.fold_in(key, 6)
    for dim, parts in cuts:
        draws = jnp.exp(jax.random.uniform(jax.random.fold_in(own, dim), (parts,), jnp.float32, smallest / len(cuts), high / len(cuts)))
        loudness = loudness * jnp.repeat(draws, shape[dim] // parts).reshape([-1 if axis == dim else 1 for axis in range(len(shape))])
    return loudness


def scatter_about(stream_key, dims, width, most, cuts=(), kind=jnp.bfloat16):
    level = block_levels(stream_key, dims, cuts, -0.22, 0.18) if cuts else 1.0
    entries = jax.random.normal(stream_key, dims, jnp.float32) * width * level
    return jnp.minimum(jnp.maximum(entries, -most), most).astype(kind)


def setup_inputs(seed: int = 0) -> dict:
    splits = jax.random.split(jax.random.key(seed), 7)
    query_proj = scatter_about(splits[0], (L, C), 1.0, 6.0, ((0, 32), (1, 16)))
    key_proj = scatter_about(splits[1], (L, C), 1.0, 6.0, ((0, 32), (1, 16)))
    value_proj = scatter_about(splits[2], (L, C), 1.0, 6.0, ((0, 32), (1, 16)))
    out_grad = scatter_about(splits[3], (L, C), 1.0, 6.0, ((0, 32), (1, 16)))
    long_filter = draw_long_filter(jax.random.fold_in(splits[6], 71), 0)
    skip_gain = scatter_about(splits[5], (C,), 1.0, 4.0, ((0, 16),), jnp.float32)
    return dict(query_proj=query_proj, key_proj=key_proj, value_proj=value_proj, out_grad=out_grad, long_filter=long_filter, skip_gain=skip_gain)


def convolve_block(operands):
    filters, forward_in, backward_in = operands
    points = 2 * L
    spectrum = jnp.fft.rfft(filters.astype(jnp.float32), n=points, axis=1)
    causal_out = jnp.fft.irfft(jnp.fft.rfft(forward_in.astype(jnp.float32), n=points, axis=1) * spectrum, n=points, axis=1)[:, :L]
    adjoint_out = jnp.fft.irfft(jnp.fft.rfft(backward_in.astype(jnp.float32), n=points, axis=1) * jnp.conj(spectrum), n=points, axis=1)[:, :L]
    return causal_out.astype(jnp.bfloat16), adjoint_out.astype(jnp.bfloat16)


def reference(query_proj, key_proj, value_proj, out_grad, long_filter, skip_gain):
    gated_kv = (key_proj.astype(jnp.float32) * value_proj.astype(jnp.float32)).astype(jnp.bfloat16)
    grad_gate = (out_grad.astype(jnp.float32) * query_proj.astype(jnp.float32)).astype(jnp.bfloat16)
    block_rows = min(64, C)
    blocks = C // block_rows
    filters = long_filter.reshape(blocks, block_rows, L)
    forward_in = gated_kv.T.reshape(blocks, block_rows, L)
    backward_in = grad_gate.T.reshape(blocks, block_rows, L)
    convolved, reflected = lax.map(convolve_block, (filters, forward_in, backward_in))
    convolved = convolved.reshape(C, L).T
    reflected = reflected.reshape(C, L).T
    summed = convolved.astype(jnp.float32) + skip_gain[None, :] * gated_kv.astype(jnp.float32)
    output = (query_proj.astype(jnp.float32) * summed).astype(jnp.bfloat16)
    query_grad = (out_grad.astype(jnp.float32) * summed).astype(jnp.bfloat16)
    grad_sum = reflected.astype(jnp.float32) + skip_gain[None, :] * grad_gate.astype(jnp.float32)
    key_grad = (grad_sum * value_proj.astype(jnp.float32)).astype(jnp.bfloat16)
    value_grad = (grad_sum * key_proj.astype(jnp.float32)).astype(jnp.bfloat16)
    return output, query_grad, key_grad, value_grad
```

```python
import jax
import jax.numpy as jnp
from jax import lax
from jax.experimental import pallas as pl
from jax.experimental.pallas import tpu as pltpu
from jax.sharding import PartitionSpec as P

CTX = 32
CH = 16
MINE = 8
ROWS = 64
BLK = 256
TAPS = 128
TBLK = 128
SEGS = 4
PER = 16
MESH = pl.DeviceIdType.MESH
F32 = jnp.float32
BF16 = jnp.bfloat16


def eye(size, flip=False):
    row = lax.broadcasted_iota(jnp.int32, (size, size), 0)
    col = lax.broadcasted_iota(jnp.int32, (size, size), 1)
    if flip:
        col = size - 1 - col
    return (row == col).astype(F32).astype(BF16)


def times_transposed(left, right):
    return lax.dot_general(left, right, (((1,), (1,)), ((), ())), preferred_element_type=F32)


def gate(left, right):
    return (left.astype(F32) * right.astype(F32)).astype(BF16)


def ctx_copy(src, dst, send_sem, recv_sem, peer):
    return pltpu.make_async_remote_copy(
        src_ref=src, dst_ref=dst, send_sem=send_sem, recv_sem=recv_sem,
        device_id={"ctx": peer}, device_id_type=MESH,
    )


def ch_copy(src, dst, send_sem, recv_sem, peer):
    return pltpu.make_async_remote_copy(
        src_ref=src, dst_ref=dst, send_sem=send_sem, recv_sem=recv_sem,
        device_id={"ch": peer}, device_id_type=MESH,
    )


def convolve_kernel(
    query, key, value, grad, taps, back,
    taps_rows, taps_send, taps_mid, taps_send2, taps_recv2, taps_wide,
    send, recv, rows_in, rows_out, back_send, blocks, shifted, lhs, acc,
    local_sem, fs1, fr1, fs2, fr2, ss, sr, bs, br,
):
    me = lax.axis_index("ctx")
    my_ch = lax.axis_index("ch")
    barrier = pltpu.get_barrier_semaphore()

    def ctx_peer(k):
        return lax.rem(me + k, CTX)

    def ch_peer(k):
        return lax.rem(my_ch + k, CH)

    @pl.loop(1, CTX)
    def _(k):
        pl.semaphore_signal(barrier, inc=1, device_id={"ctx": ctx_peer(k)}, device_id_type=MESH)

    @pl.loop(1, CH)
    def _(k):
        pl.semaphore_signal(barrier, inc=1, device_id={"ch": ch_peer(k)}, device_id_type=MESH)

    taps_rows[...] = taps[...].astype(F32).reshape(CH * CTX, MINE, 32)
    small = eye(32)

    @pl.loop(0, CTX)
    def _(p):
        tile = taps_rows[pl.ds(p, CH, stride=CTX)].reshape(CH * MINE, 32).astype(BF16)
        taps_send[p] = times_transposed(small, tile).astype(BF16)

    pl.semaphore_wait(barrier, CTX - 1 + CH - 1)

    @pl.loop(1, CTX)
    def _(k):
        p = ctx_peer(k)
        ctx_copy(taps_send.at[p], taps_mid.at[me], fs1.at[p], fr1.at[me], p).start()

    own1 = pltpu.make_async_copy(taps_send.at[me], taps_mid.at[me], local_sem.at[0])
    own1.start()

    unit = eye(BLK)
    mirror = eye(BLK, True)
    for half in range(2):
        toks = pl.ds(BLK * half, BLK)
        gated = times_transposed(unit, gate(key[toks, :], value[toks, :]))
        turned = jnp.dot(mirror, gate(grad[toks, :], query[toks, :]), preferred_element_type=F32)
        graded = times_transposed(unit, turned.astype(BF16))
        both = jnp.concatenate(
            [gated.reshape(CTX, MINE, BLK), graded.reshape(CTX, MINE, BLK)], axis=1
        )
        send[:, half] = both.astype(BF16)

    @pl.loop(1, CTX)
    def _(k):
        p = ctx_peer(k)
        ctx_copy(send.at[p], recv.at[me], ss.at[p], sr.at[me], p).start()

    own2 = pltpu.make_async_copy(send.at[me], recv.at[me], local_sem.at[1])
    own2.start()

    own1.wait()

    @pl.loop(1, CTX)
    def _(k):
        p = ctx_peer(k)
        ctx_copy(taps_send.at[p], taps_mid.at[p], fs1.at[p], fr1.at[p], p).wait_recv()

    unit_t = eye(TAPS)
    for b in range(8):
        tile = taps_mid[pl.ds(4 * b, 4)].reshape(TAPS, CH * MINE)
        turned = times_transposed(unit_t, tile)
        taps_send2[:, :, pl.ds(TAPS * b, TAPS)] = turned.reshape(CH, MINE, TAPS).astype(BF16)

    @pl.loop(1, CH)
    def _(k):
        p = ch_peer(k)
        ch_copy(taps_send2.at[p], taps_recv2.at[my_ch], fs2.at[p], fr2.at[my_ch], p).start()

    own3 = pltpu.make_async_copy(taps_send2.at[my_ch], taps_recv2.at[my_ch], local_sem.at[2])
    own3.start()
    own3.wait()

    @pl.loop(1, CH)
    def _(k):
        p = ch_peer(k)
        ch_copy(taps_send2.at[p], taps_recv2.at[p], fs2.at[p], fr2.at[p], p).wait_recv()

    for sub in range(8):
        taps_wide[:, sub] = taps_recv2[:, :, pl.ds(TAPS * sub, TAPS)].astype(F32)

    row = lax.broadcasted_iota(jnp.int32, (TAPS, TAPS), 0)
    col = lax.broadcasted_iota(jnp.int32, (TAPS, TAPS), 1)
    keep = col >= row

    @pl.loop(0, MINE)
    def _(c):
        blocks[c, pl.ds(0, TAPS), :] = jnp.zeros((TAPS, TAPS), BF16)

        def build(j, prev):
            for sub in range(8):
                line = taps_wide[j, sub, pl.ds(c, 1), :]
                wide = jnp.broadcast_to(line, (TAPS, TAPS))
                rolled = pltpu.roll(wide, 0, 1, stride=1, stride_axis=0)
                start = pl.multiple_of((j * 8 + sub + 1) * TAPS, TAPS)
                blocks[c, pl.ds(start, TAPS), :] = jnp.where(keep, rolled, prev).astype(BF16)
                prev = rolled
            return prev

        lax.fori_loop(0, CH, build, jnp.zeros((TAPS, TAPS), F32))

    own2.wait()

    @pl.loop(1, CTX)
    def _(k):
        p = ctx_peer(k)
        ctx_copy(send.at[p], recv.at[p], ss.at[p], sr.at[p], p).wait_recv()

    for half in range(2):
        part = recv[:, :, :, pl.ds(TAPS * half, TAPS)].astype(F32)
        rows_in[half] = part.reshape(ROWS * 2 * MINE, TAPS)
    blank = jnp.zeros((ROWS, TAPS), F32)
    for half in range(2):
        shifted[0, half, pl.ds(0, ROWS), :] = blank
        shifted[1, half, pl.ds(ROWS, ROWS), :] = blank

    @pl.loop(0, MINE)
    def _(c):
        for half in range(2):
            shifted[0, half, pl.ds(ROWS, ROWS), :] = rows_in[half, pl.ds(c, ROWS, stride=2 * MINE), :]
            shifted[1, half, pl.ds(0, ROWS), :] = rows_in[half, pl.ds(c + MINE, ROWS, stride=2 * MINE), :]
        for s in range(SEGS):
            n = ROWS - PER * s
            for e in range(PER):
                far = PER * s + e
                for part in range(2):
                    half = 1 - part
                    lanes = pl.ds(e * BLK + part * TAPS, TAPS)
                    lhs[s, pl.ds(0, n), lanes] = shifted[0, half, pl.ds(ROWS - e, n), :].astype(BF16)
                    lhs[s, pl.ds(n, n), lanes] = shifted[1, half, pl.ds(far, n), :].astype(BF16)
        for s in range(SEGS):
            n = ROWS - PER * s
            depth = PER * BLK
            rhs = jnp.concatenate(
                [
                    blocks[c, pl.ds(depth * s, depth), :],
                    blocks[c, pl.ds(depth * s + TAPS, depth), :],
                ],
                axis=1,
            )
            out = jnp.dot(lhs[s, pl.ds(0, 2 * n), :], rhs, preferred_element_type=F32)
            if s == 0:
                acc[...] = out
            else:
                acc[pl.ds(PER * s, n), :] += out[:n]
                acc[pl.ds(ROWS, n), :] += out[n:]
        for half in range(2):
            lanes = pl.ds(TAPS * half, TAPS)
            rows_out[half, pl.ds(c, ROWS, stride=2 * MINE), :] = acc[pl.ds(0, ROWS), lanes]
            rows_out[half, pl.ds(c + MINE, ROWS, stride=2 * MINE), :] = acc[pl.ds(ROWS, ROWS), lanes]

    for half in range(2):
        part = rows_out[half].reshape(CTX, 2, 2 * MINE, TAPS)
        back_send[:, :, :, pl.ds(TAPS * half, TAPS)] = part.astype(BF16)

    @pl.loop(1, CTX)
    def _(k):
        p = ctx_peer(k)
        ctx_copy(back_send.at[p], back.at[me], bs.at[p], br.at[me], p).start()

    own4 = pltpu.make_async_copy(back_send.at[me], back.at[me], local_sem.at[3])
    own4.start()

    @pl.loop(1, CTX)
    def _(k):
        p = ctx_peer(k)
        ctx_copy(taps_send.at[p], taps_mid.at[p], fs1.at[p], fr1.at[p], p).wait_send()
        ctx_copy(send.at[p], recv.at[p], ss.at[p], sr.at[p], p).wait_send()

    @pl.loop(1, CH)
    def _(k):
        p = ch_peer(k)
        ch_copy(taps_send2.at[p], taps_recv2.at[p], fs2.at[p], fr2.at[p], p).wait_send()

    own4.wait()

    @pl.loop(1, CTX)
    def _(k):
        p = ctx_peer(k)
        done = ctx_copy(back_send.at[p], back.at[p], bs.at[p], br.at[p], p)
        done.wait_send()
        done.wait_recv()


def finish_kernel(query, key, value, grad, gain, back, output, query_grad, key_grad, value_grad):
    unit = eye(BLK)
    mirror = eye(BLK, True)
    scale = gain[...]
    for half in range(2):
        toks = pl.ds(BLK * half, BLK)
        wide = back[:, half].astype(F32)
        conv = wide[:, :MINE].reshape(CTX * MINE, BLK).astype(BF16)
        refl = wide[:, MINE:].reshape(CTX * MINE, BLK).astype(BF16)
        q = query[toks, :].astype(F32)
        k = key[toks, :].astype(F32)
        v = value[toks, :].astype(F32)
        g = grad[toks, :].astype(F32)
        summed = times_transposed(unit, conv) + scale * (k * v).astype(BF16).astype(F32)
        output[toks, :] = (q * summed).astype(BF16)
        query_grad[toks, :] = (g * summed).astype(BF16)
        grad_sum = times_transposed(mirror, refl) + scale * (g * q).astype(BF16).astype(F32)
        key_grad[toks, :] = (grad_sum * v).astype(BF16)
        value_grad[toks, :] = (grad_sum * k).astype(BF16)


def shards(query, key, value, grad, taps, gain):
    vmem = pl.BlockSpec(memory_space=pltpu.VMEM)
    dma = pltpu.SemaphoreType.DMA
    tile = (CTX, 2, 2 * MINE, BLK)
    back = pl.pallas_call(
        convolve_kernel,
        out_shape=jax.ShapeDtypeStruct(tile, BF16),
        in_specs=[vmem] * 5,
        out_specs=vmem,
        scratch_shapes=[
            pltpu.VMEM((CH * CTX, MINE, 32), F32),
            pltpu.VMEM((CTX, 32, CH * MINE), BF16),
            pltpu.VMEM((CTX, 32, CH * MINE), BF16),
            pltpu.VMEM((CH, MINE, 1024), BF16),
            pltpu.VMEM((CH, MINE, 1024), BF16),
            pltpu.VMEM((CH, 8, MINE, TAPS), F32),
            pltpu.VMEM(tile, BF16),
            pltpu.VMEM(tile, BF16),
            pltpu.VMEM((2, ROWS * 2 * MINE, TAPS), F32),
            pltpu.VMEM((2, ROWS * 2 * MINE, TAPS), F32),
            pltpu.VMEM(tile, BF16),
            pltpu.VMEM((MINE, (TBLK + 1) * TAPS, TAPS), BF16),
            pltpu.VMEM((2, 2, 2 * ROWS, TAPS), F32),
            pltpu.VMEM((SEGS, 2 * ROWS, PER * BLK), BF16),
            pltpu.VMEM((2 * ROWS, BLK), F32),
            dma((4,)),
            dma((CTX,)), dma((CTX,)),
            dma((CH,)), dma((CH,)),
            dma((CTX,)), dma((CTX,)),
            dma((CTX,)), dma((CTX,)),
        ],
        compiler_params=pltpu.CompilerParams(
            collective_id=0, has_side_effects=True, vmem_limit_bytes=60 * 2**20
        ),
        name="convolve",
    )(query, key, value, grad, taps)
    shape = jax.ShapeDtypeStruct(query.shape, BF16)
    return pl.pallas_call(
        finish_kernel,
        out_shape=(shape,) * 4,
        in_specs=[vmem] * 6,
        out_specs=(vmem,) * 4,
        name="finish",
    )(query, key, value, grad, gain.reshape(1, -1), back)


def solution(mesh):
    placed = (
        P("ctx", "ch"),
        P("ctx", "ch"),
        P("ctx", "ch"),
        P("ctx", "ch"),
        P(None, ("ch", "ctx")),
        P("ch"),
    )
    return jax.shard_map(
        shards,
        mesh=mesh,
        in_specs=placed,
        out_specs=(P("ctx", "ch"), P("ctx", "ch"), P("ctx", "ch"), P("ctx", "ch")),
        check_vma=False,
    )
```

```python
import jax
import jax.numpy as jnp
from jax import lax
from jax.experimental import pallas as pl
from jax.experimental.pallas import tpu as pltpu
from jax.sharding import PartitionSpec as P

CTX = 32
CH = 16
MINE = 8
ROWS = 64
BLK = 256
TAPS = 128
TBLK = 128
GROUPS = 4
STEP = 32
PAIR = MINE // GROUPS
SEGS = 4
PER = 16
MESH = pl.DeviceIdType.MESH
F32 = jnp.float32
BF16 = jnp.bfloat16


def eye(size, flip=False):
    row = lax.broadcasted_iota(jnp.int32, (size, size), 0)
    col = lax.broadcasted_iota(jnp.int32, (size, size), 1)
    if flip:
        col = size - 1 - col
    return (row == col).astype(F32).astype(BF16)


def spread(size):
    row = lax.broadcasted_iota(jnp.int32, (size, size), 0)
    col = lax.broadcasted_iota(jnp.int32, (size, size), 1)
    return (row == col % CTX * MINE + col // CTX).astype(F32).astype(BF16)


def times_transposed(left, right):
    return lax.dot_general(left, right, (((1,), (1,)), ((), ())), preferred_element_type=F32)


def gate(left, right):
    return (left.astype(F32) * right.astype(F32)).astype(BF16)


def remote(src, dst, send_sem, recv_sem, ctx, ch):
    return pltpu.make_async_remote_copy(
        src_ref=src, dst_ref=dst, send_sem=send_sem, recv_sem=recv_sem,
        device_id={"ctx": ctx, "ch": ch}, device_id_type=MESH,
    )


def convolve_kernel(
    query, key, value, grad, taps, back,
    taps_mid, taps_send, taps_recv, taps_wide,
    send, recv, rows_in, rows_out, back_send, blocks, shifted, lhs, acc,
    local_sem, fs1, fr1, fs2, fr2, ss, sr, bs, br,
):
    me = lax.axis_index("ctx")
    my_ch = lax.axis_index("ch")
    across = lax.rem(my_ch + CH // 2, CH)
    barrier = pltpu.get_barrier_semaphore()

    def ctx_peer(k):
        return lax.rem(me + k, CTX)

    def ch_peer(k):
        return lax.rem(my_ch + k, CH)

    @pl.loop(0, CTX)
    def _(k):
        where = {"ctx": ctx_peer(k), "ch": across}
        pl.semaphore_signal(barrier, inc=1, device_id=where, device_id_type=MESH)

    @pl.loop(1, CH)
    def _(k):
        where = {"ctx": me, "ch": ch_peer(k)}
        pl.semaphore_signal(barrier, inc=1, device_id=where, device_id_type=MESH)

    pl.semaphore_wait(barrier, CTX + CH - 1)

    def columns(p):
        return taps.at[:, pl.ds(pl.multiple_of(p * 256, 256), 256)]

    @pl.loop(1, CH)
    def _(k):
        p = ch_peer(k)
        remote(columns(p), taps_mid.at[my_ch], fs1.at[p], fr1.at[my_ch], me, p).start()

    own = pltpu.make_async_copy(columns(my_ch), taps_mid.at[my_ch], local_sem.at[0])
    own.start()

    order = spread(BLK)
    mirror = eye(BLK, True)
    for half in range(2):
        toks = pl.ds(BLK * half, BLK)
        gated = times_transposed(order, gate(key[toks, :], value[toks, :]))
        turned = jnp.dot(mirror, gate(grad[toks, :], query[toks, :]), preferred_element_type=F32)
        graded = times_transposed(order, turned.astype(BF16))
        both = jnp.concatenate(
            [gated.reshape(CTX, MINE, BLK), graded.reshape(CTX, MINE, BLK)], axis=1
        )
        send[:, half] = both.astype(BF16)

    own.wait()

    @pl.loop(1, CH)
    def _(k):
        p = ch_peer(k)
        remote(columns(p), taps_mid.at[p], fs1.at[p], fr1.at[p], me, p).wait_recv()

    for b in range(4):
        tile = taps_mid[pl.ds(4 * b, 4)].reshape(TAPS, 256)
        turned = times_transposed(order, tile)
        taps_send[:, :, pl.ds(TAPS * b, TAPS)] = turned.reshape(CTX, MINE, TAPS).astype(BF16)

    @pl.loop(0, CTX)
    def _(k):
        p = ctx_peer(k)
        remote(taps_send.at[p], taps_recv.at[me], fs2.at[p], fr2.at[me], p, across).start()

    @pl.loop(0, CTX)
    def _(k):
        p = ctx_peer(k)
        remote(send.at[p], recv.at[me], ss.at[p], sr.at[me], p, across).start()

    @pl.loop(0, CTX)
    def _(k):
        p = ctx_peer(k)
        remote(taps_send.at[p], taps_recv.at[p], fs2.at[p], fr2.at[p], p, across).wait_recv()

    lane = lax.broadcasted_iota(jnp.int32, (MINE, TAPS), 1)
    low_half = lane < 64
    low_quarter = lane % 64 < 32

    @pl.loop(0, 8)
    def _(m):
        for k in range(4):
            a, b, c, d = [
                taps_recv[4 * m + q, :, pl.ds(TAPS * k, TAPS)].astype(F32) for q in range(4)
            ]

            def swap(x, y, low, width):
                first = jnp.where(low, x, pltpu.roll(y, width, 1))
                second = jnp.where(low, pltpu.roll(x, TAPS - width, 1), y)
                return first, second

            a, c = swap(a, c, low_half, 64)
            b, d = swap(b, d, low_half, 64)
            a, b = swap(a, b, low_quarter, 32)
            c, d = swap(c, d, low_quarter, 32)
            for s, line in enumerate((a, b, c, d)):
                taps_wide[(4 * k + s) * 8 + m] = line

    row = lax.broadcasted_iota(jnp.int32, (TAPS, TAPS), 0)
    col = lax.broadcasted_iota(jnp.int32, (TAPS, TAPS), 1)
    keep = col >= row

    @pl.loop(0, MINE)
    def _(c):
        blocks[c, pl.ds(0, TAPS), :] = jnp.zeros((TAPS, TAPS), BF16)

        def build(j, prev):
            for sub in range(STEP):
                line = taps_wide[j * STEP + sub, pl.ds(c, 1), :]
                wide = jnp.broadcast_to(line, (TAPS, TAPS))
                rolled = pltpu.roll(wide, 0, 1, stride=1, stride_axis=0)
                start = pl.multiple_of((j * STEP + sub + 1) * TAPS, TAPS)
                blocks[c, pl.ds(start, TAPS), :] = jnp.where(keep, rolled, prev).astype(BF16)
                prev = rolled
            return prev

        lax.fori_loop(0, TBLK // STEP, build, jnp.zeros((TAPS, TAPS), F32))

    @pl.loop(0, CTX)
    def _(k):
        p = ctx_peer(k)
        remote(send.at[p], recv.at[p], ss.at[p], sr.at[p], p, across).wait_recv()

    for half in range(2):
        part = recv[:, :, :, pl.ds(TAPS * half, TAPS)].astype(F32)
        rows_in[half] = part.reshape(ROWS * 2 * MINE, TAPS)
    blank = jnp.zeros((ROWS, TAPS), F32)
    for half in range(2):
        shifted[0, half, pl.ds(0, ROWS), :] = blank
        shifted[1, half, pl.ds(ROWS, ROWS), :] = blank

    @pl.loop(0, GROUPS)
    def _(group):
        @pl.loop(0, PAIR)
        def _(r):
            c = group * PAIR + r
            for half in range(2):
                shifted[0, half, pl.ds(ROWS, ROWS), :] = rows_in[half, pl.ds(c, ROWS, stride=2 * MINE), :]
                shifted[1, half, pl.ds(0, ROWS), :] = rows_in[half, pl.ds(c + MINE, ROWS, stride=2 * MINE), :]
            for s in range(SEGS):
                n = ROWS - PER * s
                for e in range(PER):
                    far = PER * s + e
                    for part in range(2):
                        half = 1 - part
                        lanes = pl.ds(e * BLK + part * TAPS, TAPS)
                        lhs[s, pl.ds(0, n), lanes] = shifted[0, half, pl.ds(ROWS - e, n), :].astype(BF16)
                        lhs[s, pl.ds(n, n), lanes] = shifted[1, half, pl.ds(far, n), :].astype(BF16)
            for s in range(SEGS):
                n = ROWS - PER * s
                depth = PER * BLK
                rhs = jnp.concatenate(
                    [
                        blocks[c, pl.ds(depth * s, depth), :],
                        blocks[c, pl.ds(depth * s + TAPS, depth), :],
                    ],
                    axis=1,
                )
                out = jnp.dot(lhs[s, pl.ds(0, 2 * n), :], rhs, preferred_element_type=F32)
                if s == 0:
                    acc[...] = out
                else:
                    acc[pl.ds(PER * s, n), :] += out[:n]
                    acc[pl.ds(ROWS, n), :] += out[n:]
            for half in range(2):
                lanes = pl.ds(TAPS * half, TAPS)
                rows_out[half, pl.ds(r, ROWS, stride=2 * PAIR), :] = acc[pl.ds(0, ROWS), lanes]
                rows_out[half, pl.ds(r + PAIR, ROWS, stride=2 * PAIR), :] = acc[pl.ds(ROWS, ROWS), lanes]

        for half in range(2):
            part = rows_out[half].reshape(CTX, 4 * PAIR, TAPS)
            back_send[group, :, :, pl.ds(TAPS * half, TAPS)] = part.astype(BF16)

        @pl.loop(0, CTX)
        def _(k):
            p = ctx_peer(k)
            remote(
                back_send.at[group, p], back.at[group, me],
                bs.at[group, p], br.at[group, me], p, across,
            ).start()

    @pl.loop(1, CH)
    def _(k):
        p = ch_peer(k)
        remote(columns(p), taps_mid.at[p], fs1.at[p], fr1.at[p], me, p).wait_send()

    @pl.loop(0, CTX)
    def _(k):
        p = ctx_peer(k)
        remote(taps_send.at[p], taps_recv.at[p], fs2.at[p], fr2.at[p], p, across).wait_send()
        remote(send.at[p], recv.at[p], ss.at[p], sr.at[p], p, across).wait_send()

    @pl.loop(0, GROUPS)
    def _(group):
        @pl.loop(0, CTX)
        def _(k):
            p = ctx_peer(k)
            done = remote(
                back_send.at[group, p], back.at[group, p],
                bs.at[group, p], br.at[group, p], p, across,
            )
            done.wait_send()
            done.wait_recv()


def finish_kernel(query, key, value, grad, gain, back, output, query_grad, key_grad, value_grad, wide):
    unit = eye(BLK)
    mirror = eye(BLK, True)
    scale = gain[...]
    for part in range(2):
        lanes = pl.ds(TAPS * part, TAPS)
        wide[part] = back[:, :, :, lanes].astype(F32).reshape(GROUPS * CTX * 4 * PAIR, TAPS)

    def rows(first):
        columns = []
        for part in range(2):
            pieces = []
            for c in range(MINE):
                start = c // PAIR * (CTX * 4 * PAIR) + first + c % PAIR
                pieces.append(wide[part, pl.ds(start, CTX, stride=4 * PAIR), :])
            columns.append(jnp.concatenate(pieces, axis=0))
        return jnp.concatenate(columns, axis=1).astype(BF16)

    for half in range(2):
        toks = pl.ds(BLK * half, BLK)
        conv = rows(2 * PAIR * half)
        refl = rows(2 * PAIR * half + PAIR)
        q = query[toks, :].astype(F32)
        k = key[toks, :].astype(F32)
        v = value[toks, :].astype(F32)
        g = grad[toks, :].astype(F32)
        summed = times_transposed(unit, conv) + scale * (k * v).astype(BF16).astype(F32)
        output[toks, :] = (q * summed).astype(BF16)
        query_grad[toks, :] = (g * summed).astype(BF16)
        grad_sum = times_transposed(mirror, refl) + scale * (g * q).astype(BF16).astype(F32)
        key_grad[toks, :] = (grad_sum * v).astype(BF16)
        value_grad[toks, :] = (grad_sum * k).astype(BF16)


def shards(query, key, value, grad, taps, gain):
    vmem = pl.BlockSpec(memory_space=pltpu.VMEM)
    dma = pltpu.SemaphoreType.DMA
    tile = (CTX, 2, 2 * MINE, BLK)
    reply = (GROUPS, CTX, 4 * PAIR, BLK)
    back = pl.pallas_call(
        convolve_kernel,
        out_shape=jax.ShapeDtypeStruct(reply, BF16),
        in_specs=[vmem] * 5,
        out_specs=vmem,
        scratch_shapes=[
            pltpu.VMEM((CH, 32, 256), BF16),
            pltpu.VMEM((CTX, MINE, 512), BF16),
            pltpu.VMEM((CTX, MINE, 512), BF16),
            pltpu.VMEM((TBLK, MINE, TAPS), F32),
            pltpu.VMEM(tile, BF16),
            pltpu.VMEM(tile, BF16),
            pltpu.VMEM((2, ROWS * 2 * MINE, TAPS), F32),
            pltpu.VMEM((2, ROWS * 2 * PAIR, TAPS), F32),
            pltpu.VMEM(reply, BF16),
            pltpu.VMEM((MINE, (TBLK + 1) * TAPS, TAPS), BF16),
            pltpu.VMEM((2, 2, 2 * ROWS, TAPS), F32),
            pltpu.VMEM((SEGS, 2 * ROWS, PER * BLK), BF16),
            pltpu.VMEM((2 * ROWS, BLK), F32),
            dma((1,)),
            dma((CH,)), dma((CH,)),
            dma((CTX,)), dma((CTX,)),
            dma((CTX,)), dma((CTX,)),
            dma((GROUPS, CTX)), dma((GROUPS, CTX)),
        ],
        compiler_params=pltpu.CompilerParams(
            collective_id=0, has_side_effects=True, vmem_limit_bytes=60 * 2**20
        ),
        name="convolve",
    )(query, key, value, grad, taps.T)
    shape = jax.ShapeDtypeStruct(query.shape, BF16)
    return pl.pallas_call(
        finish_kernel,
        out_shape=(shape,) * 4,
        in_specs=[vmem] * 6,
        out_specs=(vmem,) * 4,
        scratch_shapes=[pltpu.VMEM((2, GROUPS * CTX * 4 * PAIR, TAPS), F32)],
        name="finish",
    )(query, key, value, grad, gain.reshape(1, -1), back)


def solution(mesh):
    placed = (
        P("ctx", "ch"),
        P("ctx", "ch"),
        P("ctx", "ch"),
        P("ctx", "ch"),
        P(None, ("ch", "ctx")),
        P("ch"),
    )
    return jax.shard_map(
        shards,
        mesh=mesh,
        in_specs=placed,
        out_specs=(P("ctx", "ch"), P("ctx", "ch"), P("ctx", "ch"), P("ctx", "ch")),
        check_vma=False,
    )
```

```python
import jax
import jax.numpy as jnp
from jax import lax
from jax.experimental import pallas as pl
from jax.experimental.pallas import tpu as pltpu
from jax.sharding import PartitionSpec as P

CTX = 32
CH = 16
MINE = 8
ROWS = 64
BLK = 256
TAPS = 128
TBLK = 128
GROUPS = 4
STEP = 32
PAIR = MINE // GROUPS
SEGS = 4
PER = 16
MESH = pl.DeviceIdType.MESH
F32 = jnp.float32
BF16 = jnp.bfloat16


def eye(size, flip=False):
    row = lax.broadcasted_iota(jnp.int32, (size, size), 0)
    col = lax.broadcasted_iota(jnp.int32, (size, size), 1)
    if flip:
        col = size - 1 - col
    return (row == col).astype(F32).astype(BF16)


def spread(size):
    row = lax.broadcasted_iota(jnp.int32, (size, size), 0)
    col = lax.broadcasted_iota(jnp.int32, (size, size), 1)
    return (row == col % CTX * MINE + col // CTX).astype(F32).astype(BF16)


def times_transposed(left, right):
    return lax.dot_general(left, right, (((1,), (1,)), ((), ())), preferred_element_type=F32)


def gate(left, right):
    return (left.astype(F32) * right.astype(F32)).astype(BF16)


def remote(src, dst, send_sem, recv_sem, ctx, ch):
    return pltpu.make_async_remote_copy(
        src_ref=src, dst_ref=dst, send_sem=send_sem, recv_sem=recv_sem,
        device_id={"ctx": ctx, "ch": ch}, device_id_type=MESH,
    )


def convolve_kernel(
    query, key, value, grad, taps, back,
    taps_mid, taps_send, taps_recv, taps_wide,
    send, recv, rows_in, rows_out, back_send, near, late, shifted, lhs, acc,
    local_sem, fs1, fr1, fs2, fr2, ss, sr, bs, br,
):
    me = lax.axis_index("ctx")
    my_ch = lax.axis_index("ch")
    across = lax.rem(my_ch + CH // 2, CH)
    barrier = pltpu.get_barrier_semaphore()

    def ctx_peer(k):
        return lax.rem(me + k, CTX)

    def ch_peer(k):
        return lax.rem(my_ch + k, CH)

    @pl.loop(0, CTX)
    def _(k):
        where = {"ctx": ctx_peer(k), "ch": across}
        pl.semaphore_signal(barrier, inc=1, device_id=where, device_id_type=MESH)

    @pl.loop(1, CH)
    def _(k):
        where = {"ctx": me, "ch": ch_peer(k)}
        pl.semaphore_signal(barrier, inc=1, device_id=where, device_id_type=MESH)

    pl.semaphore_wait(barrier, CTX + CH - 1)

    def columns(p):
        return taps.at[:, pl.ds(pl.multiple_of(p * 256, 256), 256)]

    @pl.loop(1, CH)
    def _(k):
        p = ch_peer(k)
        remote(columns(p), taps_mid.at[my_ch], fs1.at[p], fr1.at[my_ch], me, p).start()

    own = pltpu.make_async_copy(columns(my_ch), taps_mid.at[my_ch], local_sem.at[0])
    own.start()

    order = spread(BLK)
    mirror = eye(BLK, True)
    for half in range(2):
        toks = pl.ds(BLK * half, BLK)
        gated = times_transposed(order, gate(key[toks, :], value[toks, :]))
        turned = jnp.dot(mirror, gate(grad[toks, :], query[toks, :]), preferred_element_type=F32)
        graded = times_transposed(order, turned.astype(BF16))
        both = jnp.concatenate(
            [gated.reshape(CTX, MINE, BLK), graded.reshape(CTX, MINE, BLK)], axis=1
        )
        send[:, half] = both.astype(BF16)

    own.wait()

    @pl.loop(1, CH)
    def _(k):
        p = ch_peer(k)
        remote(columns(p), taps_mid.at[p], fs1.at[p], fr1.at[p], me, p).wait_recv()

    for b in range(4):
        tile = taps_mid[pl.ds(4 * b, 4)].reshape(TAPS, 256)
        turned = times_transposed(order, tile)
        taps_send[:, :, pl.ds(TAPS * b, TAPS)] = turned.reshape(CTX, MINE, TAPS).astype(BF16)

    @pl.loop(0, CTX)
    def _(k):
        p = ctx_peer(k)
        remote(taps_send.at[p], taps_recv.at[me], fs2.at[p], fr2.at[me], p, across).start()

    @pl.loop(0, CTX)
    def _(k):
        p = ctx_peer(k)
        remote(send.at[p], recv.at[me], ss.at[p], sr.at[me], p, across).start()

    @pl.loop(0, CTX)
    def _(k):
        p = ctx_peer(k)
        remote(taps_send.at[p], taps_recv.at[p], fs2.at[p], fr2.at[p], p, across).wait_recv()

    lane = lax.broadcasted_iota(jnp.int32, (MINE, TAPS), 1)
    low_half = lane < 64
    low_quarter = lane % 64 < 32

    @pl.loop(0, 8)
    def _(m):
        for k in range(4):
            a, b, c, d = [
                taps_recv[4 * m + q, :, pl.ds(TAPS * k, TAPS)].astype(F32) for q in range(4)
            ]

            def swap(x, y, low, width):
                first = jnp.where(low, x, pltpu.roll(y, width, 1))
                second = jnp.where(low, pltpu.roll(x, TAPS - width, 1), y)
                return first, second

            a, c = swap(a, c, low_half, 64)
            b, d = swap(b, d, low_half, 64)
            a, b = swap(a, b, low_quarter, 32)
            c, d = swap(c, d, low_quarter, 32)
            for s, line in enumerate((a, b, c, d)):
                taps_wide[(4 * k + s) * 8 + m] = line

    row = lax.broadcasted_iota(jnp.int32, (TAPS, TAPS), 0)
    col = lax.broadcasted_iota(jnp.int32, (TAPS, TAPS), 1)
    keep = col >= row

    def build(blocks, slot, c, j, prev):
        for sub in range(STEP):
            line = taps_wide[j * STEP + sub, pl.ds(c, 1), :]
            wide = jnp.broadcast_to(line, (TAPS, TAPS))
            rolled = pltpu.roll(wide, 0, 1, stride=1, stride_axis=0)
            start = (j * STEP + sub + 1) * TAPS
            if not isinstance(j, int):
                start = pl.multiple_of(start, TAPS)
            blocks[slot, pl.ds(start, TAPS), :] = jnp.where(keep, rolled, prev).astype(BF16)
            prev = rolled
        return prev

    @pl.loop(0, MINE // 2)
    def _(c):
        near[c, pl.ds(0, TAPS), :] = jnp.zeros((TAPS, TAPS), BF16)
        late[c, pl.ds(0, TAPS), :] = jnp.zeros((TAPS, TAPS), BF16)
        lax.fori_loop(
            0, TBLK // STEP, lambda j, prev: build(near, c, c, j, prev), jnp.zeros((TAPS, TAPS), F32)
        )

    @pl.loop(0, CTX)
    def _(k):
        p = ctx_peer(k)
        remote(send.at[p], recv.at[p], ss.at[p], sr.at[p], p, across).wait_recv()

    for half in range(2):
        part = recv[:, :, :, pl.ds(TAPS * half, TAPS)].astype(F32)
        rows_in[half] = part.reshape(ROWS * 2 * MINE, TAPS)
    blank = jnp.zeros((ROWS, TAPS), F32)
    for half in range(2):
        shifted[0, half, pl.ds(0, ROWS), :] = blank
        shifted[1, half, pl.ds(ROWS, ROWS), :] = blank

    def channel(c, r, blocks, slot, ahead):
        for half in range(2):
            shifted[0, half, pl.ds(ROWS, ROWS), :] = rows_in[half, pl.ds(c, ROWS, stride=2 * MINE), :]
            shifted[1, half, pl.ds(0, ROWS), :] = rows_in[half, pl.ds(c + MINE, ROWS, stride=2 * MINE), :]
        for s in range(SEGS):
            n = ROWS - PER * s
            for e in range(PER):
                far = PER * s + e
                for part in range(2):
                    half = 1 - part
                    lanes = pl.ds(e * BLK + part * TAPS, TAPS)
                    lhs[s, pl.ds(0, n), lanes] = shifted[0, half, pl.ds(ROWS - e, n), :].astype(BF16)
                    lhs[s, pl.ds(n, n), lanes] = shifted[1, half, pl.ds(far, n), :].astype(BF16)
        prev = jnp.zeros((TAPS, TAPS), F32)
        for s in range(SEGS):
            n = ROWS - PER * s
            depth = PER * BLK
            if ahead:
                prev = build(late, slot, c + MINE // 2, s, prev)
            rhs = jnp.concatenate(
                [
                    blocks[slot, pl.ds(depth * s, depth), :],
                    blocks[slot, pl.ds(depth * s + TAPS, depth), :],
                ],
                axis=1,
            )
            out = jnp.dot(lhs[s, pl.ds(0, 2 * n), :], rhs, preferred_element_type=F32)
            if s == 0:
                acc[...] = out
            else:
                acc[pl.ds(PER * s, n), :] += out[:n]
                acc[pl.ds(ROWS, n), :] += out[n:]
        for half in range(2):
            lanes = pl.ds(TAPS * half, TAPS)
            rows_out[half, pl.ds(r, ROWS, stride=2 * PAIR), :] = acc[pl.ds(0, ROWS), lanes]
            rows_out[half, pl.ds(r + PAIR, ROWS, stride=2 * PAIR), :] = acc[pl.ds(ROWS, ROWS), lanes]

    def reply(group):
        for half in range(2):
            part = rows_out[half].reshape(CTX, 4 * PAIR, TAPS)
            back_send[group, :, :, pl.ds(TAPS * half, TAPS)] = part.astype(BF16)

        @pl.loop(0, CTX)
        def _(k):
            p = ctx_peer(k)
            remote(
                back_send.at[group, p], back.at[group, me],
                bs.at[group, p], br.at[group, me], p, across,
            ).start()

    @pl.loop(0, GROUPS // 2)
    def _(group):
        @pl.loop(0, PAIR)
        def _(r):
            c = group * PAIR + r
            channel(c, r, near, c, True)

        reply(group)

    @pl.loop(GROUPS // 2, GROUPS)
    def _(group):
        @pl.loop(0, PAIR)
        def _(r):
            c = group * PAIR + r
            channel(c, r, late, c - MINE // 2, False)

        reply(group)

    @pl.loop(1, CH)
    def _(k):
        p = ch_peer(k)
        remote(columns(p), taps_mid.at[p], fs1.at[p], fr1.at[p], me, p).wait_send()

    @pl.loop(0, CTX)
    def _(k):
        p = ctx_peer(k)
        remote(taps_send.at[p], taps_recv.at[p], fs2.at[p], fr2.at[p], p, across).wait_send()
        remote(send.at[p], recv.at[p], ss.at[p], sr.at[p], p, across).wait_send()

    @pl.loop(0, GROUPS)
    def _(group):
        @pl.loop(0, CTX)
        def _(k):
            p = ctx_peer(k)
            done = remote(
                back_send.at[group, p], back.at[group, p],
                bs.at[group, p], br.at[group, p], p, across,
            )
            done.wait_send()
            done.wait_recv()


def finish_kernel(query, key, value, grad, gain, back, output, query_grad, key_grad, value_grad, wide):
    unit = eye(BLK)
    mirror = eye(BLK, True)
    scale = gain[...]
    for part in range(2):
        lanes = pl.ds(TAPS * part, TAPS)
        wide[part] = back[:, :, :, lanes].astype(F32).reshape(GROUPS * CTX * 4 * PAIR, TAPS)

    def rows(first):
        columns = []
        for part in range(2):
            pieces = []
            for c in range(MINE):
                start = c // PAIR * (CTX * 4 * PAIR) + first + c % PAIR
                pieces.append(wide[part, pl.ds(start, CTX, stride=4 * PAIR), :])
            columns.append(jnp.concatenate(pieces, axis=0))
        return jnp.concatenate(columns, axis=1).astype(BF16)

    for half in range(2):
        toks = pl.ds(BLK * half, BLK)
        conv = rows(2 * PAIR * half)
        refl = rows(2 * PAIR * half + PAIR)
        q = query[toks, :].astype(F32)
        k = key[toks, :].astype(F32)
        v = value[toks, :].astype(F32)
        g = grad[toks, :].astype(F32)
        summed = times_transposed(unit, conv) + scale * (k * v).astype(BF16).astype(F32)
        output[toks, :] = (q * summed).astype(BF16)
        query_grad[toks, :] = (g * summed).astype(BF16)
        grad_sum = times_transposed(mirror, refl) + scale * (g * q).astype(BF16).astype(F32)
        key_grad[toks, :] = (grad_sum * v).astype(BF16)
        value_grad[toks, :] = (grad_sum * k).astype(BF16)


def shards(query, key, value, grad, taps, gain):
    vmem = pl.BlockSpec(memory_space=pltpu.VMEM)
    dma = pltpu.SemaphoreType.DMA
    tile = (CTX, 2, 2 * MINE, BLK)
    reply = (GROUPS, CTX, 4 * PAIR, BLK)
    back = pl.pallas_call(
        convolve_kernel,
        out_shape=jax.ShapeDtypeStruct(reply, BF16),
        in_specs=[vmem] * 5,
        out_specs=vmem,
        scratch_shapes=[
            pltpu.VMEM((CH, 32, 256), BF16),
            pltpu.VMEM((CTX, MINE, 512), BF16),
            pltpu.VMEM((CTX, MINE, 512), BF16),
            pltpu.VMEM((TBLK, MINE, TAPS), F32),
            pltpu.VMEM(tile, BF16),
            pltpu.VMEM(tile, BF16),
            pltpu.VMEM((2, ROWS * 2 * MINE, TAPS), F32),
            pltpu.VMEM((2, ROWS * 2 * PAIR, TAPS), F32),
            pltpu.VMEM(reply, BF16),
            pltpu.VMEM((MINE // 2, (TBLK + 1) * TAPS, TAPS), BF16),
            pltpu.VMEM((MINE // 2, (TBLK + 1) * TAPS, TAPS), BF16),
            pltpu.VMEM((2, 2, 2 * ROWS, TAPS), F32),
            pltpu.VMEM((SEGS, 2 * ROWS, PER * BLK), BF16),
            pltpu.VMEM((2 * ROWS, BLK), F32),
            dma((1,)),
            dma((CH,)), dma((CH,)),
            dma((CTX,)), dma((CTX,)),
            dma((CTX,)), dma((CTX,)),
            dma((GROUPS, CTX)), dma((GROUPS, CTX)),
        ],
        compiler_params=pltpu.CompilerParams(
            collective_id=0, has_side_effects=True, vmem_limit_bytes=60 * 2**20
        ),
        name="convolve",
    )(query, key, value, grad, taps.T)
    shape = jax.ShapeDtypeStruct(query.shape, BF16)
    return pl.pallas_call(
        finish_kernel,
        out_shape=(shape,) * 4,
        in_specs=[vmem] * 6,
        out_specs=(vmem,) * 4,
        scratch_shapes=[pltpu.VMEM((2, GROUPS * CTX * 4 * PAIR, TAPS), F32)],
        name="finish",
    )(query, key, value, grad, gain.reshape(1, -1), back)


def solution(mesh):
    placed = (
        P("ctx", "ch"),
        P("ctx", "ch"),
        P("ctx", "ch"),
        P("ctx", "ch"),
        P(None, ("ch", "ctx")),
        P("ch"),
    )
    return jax.shard_map(
        shards,
        mesh=mesh,
        in_specs=placed,
        out_specs=(P("ctx", "ch"), P("ctx", "ch"), P("ctx", "ch"), P("ctx", "ch")),
        check_vma=False,
    )
```

```python
import jax
import jax.numpy as jnp
from jax import lax
from jax.experimental import pallas as pl
from jax.experimental.pallas import tpu as pltpu
from jax.sharding import PartitionSpec as P

CTX = 32
CH = 16
MINE = 8
ROWS = 64
BLK = 256
TAPS = 128
TBLK = 128
GROUPS = 4
STEP = 32
PAIR = MINE // GROUPS
SEGS = 4
PER = 16
MESH = pl.DeviceIdType.MESH
F32 = jnp.float32
BF16 = jnp.bfloat16


def eye(size, flip=False):
    row = lax.broadcasted_iota(jnp.int32, (size, size), 0)
    col = lax.broadcasted_iota(jnp.int32, (size, size), 1)
    if flip:
        col = size - 1 - col
    return (row == col).astype(F32).astype(BF16)


def spread(size):
    row = lax.broadcasted_iota(jnp.int32, (size, size), 0)
    col = lax.broadcasted_iota(jnp.int32, (size, size), 1)
    return (row == col % CTX * MINE + col // CTX).astype(F32).astype(BF16)


def times_transposed(left, right):
    return lax.dot_general(left, right, (((1,), (1,)), ((), ())), preferred_element_type=F32)


def gate(left, right):
    return (left.astype(F32) * right.astype(F32)).astype(BF16)


def remote(src, dst, send_sem, recv_sem, ctx, ch):
    return pltpu.make_async_remote_copy(
        src_ref=src, dst_ref=dst, send_sem=send_sem, recv_sem=recv_sem,
        device_id={"ctx": ctx, "ch": ch}, device_id_type=MESH,
    )


def convolve_kernel(
    query_in, key_in, value_in, grad_in, taps_in, back,
    query, key, value, grad, taps, taps_mid, taps_send, taps_recv, taps_wide,
    send, recv, rows_in, rows_out, back_send, near, late, shifted, lhs, acc,
    local_sem, in_sem, fs1, fr1, fs2, fr2, ss, sr, bs, br,
):
    me = lax.axis_index("ctx")
    my_ch = lax.axis_index("ch")
    across = lax.rem(my_ch + CH // 2, CH)
    barrier = pltpu.get_barrier_semaphore()

    def ctx_peer(k):
        return lax.rem(me + k, CTX)

    def ch_peer(k):
        return lax.rem(my_ch + k, CH)

    @pl.loop(0, CTX)
    def _(k):
        where = {"ctx": ctx_peer(k), "ch": across}
        pl.semaphore_signal(barrier, inc=1, device_id=where, device_id_type=MESH)

    @pl.loop(1, CH)
    def _(k):
        where = {"ctx": me, "ch": ch_peer(k)}
        pl.semaphore_signal(barrier, inc=1, device_id=where, device_id_type=MESH)

    loads = [
        pltpu.make_async_copy(src, dst, in_sem.at[index])
        for index, (src, dst) in enumerate(
            ((taps_in, taps), (key_in, key), (value_in, value), (grad_in, grad), (query_in, query))
        )
    ]
    for load in loads:
        load.start()
    loads[0].wait()
    pl.semaphore_wait(barrier, CTX + CH - 1)

    def columns(p):
        return taps.at[:, pl.ds(pl.multiple_of(p * 256, 256), 256)]

    @pl.loop(1, CH)
    def _(k):
        p = ch_peer(k)
        remote(columns(p), taps_mid.at[my_ch], fs1.at[p], fr1.at[my_ch], me, p).start()

    own = pltpu.make_async_copy(columns(my_ch), taps_mid.at[my_ch], local_sem.at[0])
    own.start()

    for load in loads[1:]:
        load.wait()
    order = spread(BLK)
    mirror = eye(BLK, True)
    for half in range(2):
        toks = pl.ds(BLK * half, BLK)
        gated = times_transposed(order, gate(key[toks, :], value[toks, :]))
        turned = jnp.dot(mirror, gate(grad[toks, :], query[toks, :]), preferred_element_type=F32)
        graded = times_transposed(order, turned.astype(BF16))
        both = jnp.concatenate(
            [gated.reshape(CTX, MINE, BLK), graded.reshape(CTX, MINE, BLK)], axis=1
        )
        send[:, half] = both.astype(BF16)

    own.wait()

    @pl.loop(1, CH)
    def _(k):
        p = ch_peer(k)
        remote(columns(p), taps_mid.at[p], fs1.at[p], fr1.at[p], me, p).wait_recv()

    for b in range(4):
        tile = taps_mid[pl.ds(4 * b, 4)].reshape(TAPS, 256)
        turned = times_transposed(order, tile)
        taps_send[:, :, pl.ds(TAPS * b, TAPS)] = turned.reshape(CTX, MINE, TAPS).astype(BF16)

    @pl.loop(0, CTX)
    def _(k):
        p = ctx_peer(k)
        remote(taps_send.at[p], taps_recv.at[me], fs2.at[p], fr2.at[me], p, across).start()

    @pl.loop(0, CTX)
    def _(k):
        p = ctx_peer(k)
        remote(send.at[p], recv.at[me], ss.at[p], sr.at[me], p, across).start()

    @pl.loop(0, CTX)
    def _(k):
        p = ctx_peer(k)
        remote(taps_send.at[p], taps_recv.at[p], fs2.at[p], fr2.at[p], p, across).wait_recv()

    lane = lax.broadcasted_iota(jnp.int32, (MINE, TAPS), 1)
    low_half = lane < 64
    low_quarter = lane % 64 < 32

    @pl.loop(0, 8)
    def _(m):
        for k in range(4):
            a, b, c, d = [
                taps_recv[4 * m + q, :, pl.ds(TAPS * k, TAPS)].astype(F32) for q in range(4)
            ]

            def swap(x, y, low, width):
                first = jnp.where(low, x, pltpu.roll(y, width, 1))
                second = jnp.where(low, pltpu.roll(x, TAPS - width, 1), y)
                return first, second

            a, c = swap(a, c, low_half, 64)
            b, d = swap(b, d, low_half, 64)
            a, b = swap(a, b, low_quarter, 32)
            c, d = swap(c, d, low_quarter, 32)
            for s, line in enumerate((a, b, c, d)):
                taps_wide[(4 * k + s) * 8 + m] = line

    row = lax.broadcasted_iota(jnp.int32, (TAPS, TAPS), 0)
    col = lax.broadcasted_iota(jnp.int32, (TAPS, TAPS), 1)
    keep = col >= row

    def build(blocks, slot, c, j, prev):
        for sub in range(STEP):
            line = taps_wide[j * STEP + sub, pl.ds(c, 1), :]
            wide = jnp.broadcast_to(line, (TAPS, TAPS))
            rolled = pltpu.roll(wide, 0, 1, stride=1, stride_axis=0)
            start = (j * STEP + sub + 1) * TAPS
            if not isinstance(j, int):
                start = pl.multiple_of(start, TAPS)
            blocks[slot, pl.ds(start, TAPS), :] = jnp.where(keep, rolled, prev).astype(BF16)
            prev = rolled
        return prev

    @pl.loop(0, MINE // 2)
    def _(c):
        near[c, pl.ds(0, TAPS), :] = jnp.zeros((TAPS, TAPS), BF16)
        late[c, pl.ds(0, TAPS), :] = jnp.zeros((TAPS, TAPS), BF16)
        lax.fori_loop(
            0, TBLK // STEP, lambda j, prev: build(near, c, c, j, prev), jnp.zeros((TAPS, TAPS), F32)
        )

    @pl.loop(0, CTX)
    def _(k):
        p = ctx_peer(k)
        remote(send.at[p], recv.at[p], ss.at[p], sr.at[p], p, across).wait_recv()

    for half in range(2):
        part = recv[:, :, :, pl.ds(TAPS * half, TAPS)].astype(F32)
        rows_in[half] = part.reshape(ROWS * 2 * MINE, TAPS)
    blank = jnp.zeros((ROWS, TAPS), F32)
    for half in range(2):
        shifted[0, half, pl.ds(0, ROWS), :] = blank
        shifted[1, half, pl.ds(ROWS, ROWS), :] = blank

    def channel(c, r, blocks, slot, ahead):
        for half in range(2):
            shifted[0, half, pl.ds(ROWS, ROWS), :] = rows_in[half, pl.ds(c, ROWS, stride=2 * MINE), :]
            shifted[1, half, pl.ds(0, ROWS), :] = rows_in[half, pl.ds(c + MINE, ROWS, stride=2 * MINE), :]
        for s in range(SEGS):
            n = ROWS - PER * s
            for e in range(PER):
                far = PER * s + e
                for part in range(2):
                    half = 1 - part
                    lanes = pl.ds(e * BLK + part * TAPS, TAPS)
                    lhs[s, pl.ds(0, n), lanes] = shifted[0, half, pl.ds(ROWS - e, n), :].astype(BF16)
                    lhs[s, pl.ds(n, n), lanes] = shifted[1, half, pl.ds(far, n), :].astype(BF16)
        prev = jnp.zeros((TAPS, TAPS), F32)
        for s in range(SEGS):
            n = ROWS - PER * s
            depth = PER * BLK
            if ahead:
                prev = build(late, slot, c + MINE // 2, s, prev)
            rhs = jnp.concatenate(
                [
                    blocks[slot, pl.ds(depth * s, depth), :],
                    blocks[slot, pl.ds(depth * s + TAPS, depth), :],
                ],
                axis=1,
            )
            out = jnp.dot(lhs[s, pl.ds(0, 2 * n), :], rhs, preferred_element_type=F32)
            if s == 0:
                acc[...] = out
            else:
                acc[pl.ds(PER * s, n), :] += out[:n]
                acc[pl.ds(ROWS, n), :] += out[n:]
        for half in range(2):
            lanes = pl.ds(TAPS * half, TAPS)
            rows_out[half, pl.ds(r, ROWS, stride=2 * PAIR), :] = acc[pl.ds(0, ROWS), lanes]
            rows_out[half, pl.ds(r + PAIR, ROWS, stride=2 * PAIR), :] = acc[pl.ds(ROWS, ROWS), lanes]

    def reply(group):
        for half in range(2):
            part = rows_out[half].reshape(CTX, 4 * PAIR, TAPS)
            back_send[group, :, :, pl.ds(TAPS * half, TAPS)] = part.astype(BF16)

        @pl.loop(0, CTX)
        def _(k):
            p = ctx_peer(k)
            remote(
                back_send.at[group, p], back.at[group, me],
                bs.at[group, p], br.at[group, me], p, across,
            ).start()

    @pl.loop(0, GROUPS // 2)
    def _(group):
        @pl.loop(0, PAIR)
        def _(r):
            c = group * PAIR + r
            channel(c, r, near, c, True)

        reply(group)

    @pl.loop(GROUPS // 2, GROUPS)
    def _(group):
        @pl.loop(0, PAIR)
        def _(r):
            c = group * PAIR + r
            channel(c, r, late, c - MINE // 2, False)

        reply(group)

    @pl.loop(1, CH)
    def _(k):
        p = ch_peer(k)
        remote(columns(p), taps_mid.at[p], fs1.at[p], fr1.at[p], me, p).wait_send()

    @pl.loop(0, CTX)
    def _(k):
        p = ctx_peer(k)
        remote(taps_send.at[p], taps_recv.at[p], fs2.at[p], fr2.at[p], p, across).wait_send()
        remote(send.at[p], recv.at[p], ss.at[p], sr.at[p], p, across).wait_send()

    @pl.loop(0, GROUPS)
    def _(group):
        @pl.loop(0, CTX)
        def _(k):
            p = ctx_peer(k)
            done = remote(
                back_send.at[group, p], back.at[group, p],
                bs.at[group, p], br.at[group, p], p, across,
            )
            done.wait_send()
            done.wait_recv()


def finish_kernel(query, key, value, grad, gain, back, output, query_grad, key_grad, value_grad, wide):
    unit = eye(BLK)
    mirror = eye(BLK, True)
    scale = gain[...]
    for part in range(2):
        lanes = pl.ds(TAPS * part, TAPS)
        wide[part] = back[:, :, :, lanes].astype(F32).reshape(GROUPS * CTX * 4 * PAIR, TAPS)

    def rows(first):
        columns = []
        for part in range(2):
            pieces = []
            for c in range(MINE):
                start = c // PAIR * (CTX * 4 * PAIR) + first + c % PAIR
                pieces.append(wide[part, pl.ds(start, CTX, stride=4 * PAIR), :])
            columns.append(jnp.concatenate(pieces, axis=0))
        return jnp.concatenate(columns, axis=1).astype(BF16)

    for half in range(2):
        toks = pl.ds(BLK * half, BLK)
        conv = rows(2 * PAIR * half)
        refl = rows(2 * PAIR * half + PAIR)
        q = query[toks, :].astype(F32)
        k = key[toks, :].astype(F32)
        v = value[toks, :].astype(F32)
        g = grad[toks, :].astype(F32)
        summed = times_transposed(unit, conv) + scale * (k * v).astype(BF16).astype(F32)
        output[toks, :] = (q * summed).astype(BF16)
        query_grad[toks, :] = (g * summed).astype(BF16)
        grad_sum = times_transposed(mirror, refl) + scale * (g * q).astype(BF16).astype(F32)
        key_grad[toks, :] = (grad_sum * v).astype(BF16)
        value_grad[toks, :] = (grad_sum * k).astype(BF16)


def shards(query, key, value, grad, taps, gain):
    vmem = pl.BlockSpec(memory_space=pltpu.VMEM)
    anywhere = pl.BlockSpec(memory_space=pl.ANY)
    dma = pltpu.SemaphoreType.DMA
    tile = (CTX, 2, 2 * MINE, BLK)
    reply = (GROUPS, CTX, 4 * PAIR, BLK)
    back = pl.pallas_call(
        convolve_kernel,
        out_shape=jax.ShapeDtypeStruct(reply, BF16),
        in_specs=[anywhere] * 5,
        out_specs=anywhere,
        scratch_shapes=[
            pltpu.VMEM(query.shape, BF16),
            pltpu.VMEM(query.shape, BF16),
            pltpu.VMEM(query.shape, BF16),
            pltpu.VMEM(query.shape, BF16),
            pltpu.VMEM((32, CH * 256), BF16),
            pltpu.VMEM((CH, 32, 256), BF16),
            pltpu.VMEM((CTX, MINE, 512), BF16),
            pltpu.VMEM((CTX, MINE, 512), BF16),
            pltpu.VMEM((TBLK, MINE, TAPS), F32),
            pltpu.VMEM(tile, BF16),
            pltpu.VMEM(tile, BF16),
            pltpu.VMEM((2, ROWS * 2 * MINE, TAPS), F32),
            pltpu.VMEM((2, ROWS * 2 * PAIR, TAPS), F32),
            pltpu.VMEM(reply, BF16),
            pltpu.VMEM((MINE // 2, (TBLK + 1) * TAPS, TAPS), BF16),
            pltpu.VMEM((MINE // 2, (TBLK + 1) * TAPS, TAPS), BF16),
            pltpu.VMEM((2, 2, 2 * ROWS, TAPS), F32),
            pltpu.VMEM((SEGS, 2 * ROWS, PER * BLK), BF16),
            pltpu.VMEM((2 * ROWS, BLK), F32),
            dma((1,)), dma((5,)),
            dma((CH,)), dma((CH,)),
            dma((CTX,)), dma((CTX,)),
            dma((CTX,)), dma((CTX,)),
            dma((GROUPS, CTX)), dma((GROUPS, CTX)),
        ],
        compiler_params=pltpu.CompilerParams(
            collective_id=0, has_side_effects=True, vmem_limit_bytes=60 * 2**20
        ),
        name="convolve",
    )(query, key, value, grad, taps.T)
    shape = jax.ShapeDtypeStruct(query.shape, BF16)
    return pl.pallas_call(
        finish_kernel,
        out_shape=(shape,) * 4,
        in_specs=[vmem] * 6,
        out_specs=(vmem,) * 4,
        scratch_shapes=[pltpu.VMEM((2, GROUPS * CTX * 4 * PAIR, TAPS), F32)],
        name="finish",
    )(query, key, value, grad, gain.reshape(1, -1), back)


def solution(mesh):
    placed = (
        P("ctx", "ch"),
        P("ctx", "ch"),
        P("ctx", "ch"),
        P("ctx", "ch"),
        P(None, ("ch", "ctx")),
        P("ch"),
    )
    return jax.shard_map(
        shards,
        mesh=mesh,
        in_specs=placed,
        out_specs=(P("ctx", "ch"), P("ctx", "ch"), P("ctx", "ch"), P("ctx", "ch")),
        check_vma=False,
    )
```

```python
import jax
import jax.numpy as jnp
from jax import lax
from jax.experimental import pallas as pl
from jax.experimental.pallas import tpu as pltpu
from jax.sharding import PartitionSpec as P

CTX = 32
CH = 16
MINE = 8
ROWS = 64
BLK = 256
TAPS = 128
TBLK = 128
GROUPS = 4
STEP = 32
PAIR = MINE // GROUPS
SEGS = 4
PER = 16
MESH = pl.DeviceIdType.MESH
F32 = jnp.float32
BF16 = jnp.bfloat16


def eye(size, flip=False):
    row = lax.broadcasted_iota(jnp.int32, (size, size), 0)
    col = lax.broadcasted_iota(jnp.int32, (size, size), 1)
    if flip:
        col = size - 1 - col
    return (row == col).astype(F32).astype(BF16)


def spread(size):
    row = lax.broadcasted_iota(jnp.int32, (size, size), 0)
    col = lax.broadcasted_iota(jnp.int32, (size, size), 1)
    return (row == col % CTX * MINE + col // CTX).astype(F32).astype(BF16)


def times_transposed(left, right):
    return lax.dot_general(left, right, (((1,), (1,)), ((), ())), preferred_element_type=F32)


def gate(left, right):
    return (left.astype(F32) * right.astype(F32)).astype(BF16)


def remote(src, dst, send_sem, recv_sem, ctx, ch):
    return pltpu.make_async_remote_copy(
        src_ref=src, dst_ref=dst, send_sem=send_sem, recv_sem=recv_sem,
        device_id={"ctx": ctx, "ch": ch}, device_id_type=MESH,
    )


def convolve_kernel(
    query_in, key_in, value_in, grad_in, taps_in, back,
    query, key, value, grad, taps, taps_mid, taps_send, taps_recv, taps_wide,
    send, recv, rows_in, rows_out, back_send, near, late, shifted, lhs, acc,
    local_sem, in_sem, fs1, fr1, fs2, fr2, ss, sr, bs, br,
):
    me = lax.axis_index("ctx")
    my_ch = lax.axis_index("ch")
    across = lax.rem(my_ch + CH // 2, CH)
    barrier = pltpu.get_barrier_semaphore()

    def ctx_peer(k):
        return lax.rem(me + k, CTX)

    def ch_peer(k):
        return lax.rem(my_ch + k, CH)

    @pl.loop(0, CTX)
    def _(k):
        where = {"ctx": ctx_peer(k), "ch": across}
        pl.semaphore_signal(barrier, inc=1, device_id=where, device_id_type=MESH)

    @pl.loop(1, CH)
    def _(k):
        where = {"ctx": me, "ch": ch_peer(k)}
        pl.semaphore_signal(barrier, inc=1, device_id=where, device_id_type=MESH)

    loads = [
        pltpu.make_async_copy(src, dst, in_sem.at[index])
        for index, (src, dst) in enumerate(
            ((taps_in, taps), (key_in, key), (value_in, value), (grad_in, grad), (query_in, query))
        )
    ]
    for load in loads:
        load.start()
    loads[0].wait()
    pl.semaphore_wait(barrier, CTX + CH - 1)

    def columns(p):
        start = p * 256
        if not isinstance(p, int):
            start = pl.multiple_of(start, 256)
        return taps.at[:, pl.ds(start, 256)]

    @pl.loop(1, CH)
    def _(k):
        p = ch_peer(k)
        remote(columns(p), taps_mid.at[my_ch], fs1.at[p], fr1.at[my_ch], me, p).start()

    own = pltpu.make_async_copy(columns(my_ch), taps_mid.at[my_ch], local_sem.at[0])
    own.start()

    for load in loads[1:]:
        load.wait()
    order = spread(BLK)
    mirror = eye(BLK, True)
    for half in range(2):
        toks = pl.ds(BLK * half, BLK)
        gated = times_transposed(order, gate(key[toks, :], value[toks, :]))
        turned = jnp.dot(mirror, gate(grad[toks, :], query[toks, :]), preferred_element_type=F32)
        graded = times_transposed(order, turned.astype(BF16))
        both = jnp.concatenate(
            [gated.reshape(CTX, MINE, BLK), graded.reshape(CTX, MINE, BLK)], axis=1
        )
        send[:, half] = both.astype(BF16)

    own.wait()

    for b in range(4):
        for p in range(4 * b, 4 * b + 4):

            @pl.when(my_ch != p)
            def _(p=p):
                remote(columns(p), taps_mid.at[p], fs1.at[p], fr1.at[p], me, p).wait_recv()

        tile = taps_mid[pl.ds(4 * b, 4)].reshape(TAPS, 256)
        turned = times_transposed(order, tile)
        taps_send[:, :, pl.ds(TAPS * b, TAPS)] = turned.reshape(CTX, MINE, TAPS).astype(BF16)

    @pl.loop(0, CTX)
    def _(k):
        p = ctx_peer(k)
        remote(taps_send.at[p], taps_recv.at[me], fs2.at[p], fr2.at[me], p, across).start()

    @pl.loop(0, CTX)
    def _(k):
        p = ctx_peer(k)
        remote(send.at[p], recv.at[me], ss.at[p], sr.at[me], p, across).start()

    lane = lax.broadcasted_iota(jnp.int32, (MINE, TAPS), 1)
    low_half = lane < 64
    low_quarter = lane % 64 < 32

    @pl.loop(0, 8)
    def _(m):
        for q in range(4):
            p = 4 * m + q
            remote(taps_send.at[p], taps_recv.at[p], fs2.at[p], fr2.at[p], p, across).wait_recv()
        for k in range(4):
            a, b, c, d = [
                taps_recv[4 * m + q, :, pl.ds(TAPS * k, TAPS)].astype(F32) for q in range(4)
            ]

            def swap(x, y, low, width):
                first = jnp.where(low, x, pltpu.roll(y, width, 1))
                second = jnp.where(low, pltpu.roll(x, TAPS - width, 1), y)
                return first, second

            a, c = swap(a, c, low_half, 64)
            b, d = swap(b, d, low_half, 64)
            a, b = swap(a, b, low_quarter, 32)
            c, d = swap(c, d, low_quarter, 32)
            for s, line in enumerate((a, b, c, d)):
                taps_wide[(4 * k + s) * 8 + m] = line

    row = lax.broadcasted_iota(jnp.int32, (TAPS, TAPS), 0)
    col = lax.broadcasted_iota(jnp.int32, (TAPS, TAPS), 1)
    keep = col >= row

    def build(blocks, slot, c, j, prev):
        for sub in range(STEP):
            line = taps_wide[j * STEP + sub, pl.ds(c, 1), :]
            wide = jnp.broadcast_to(line, (TAPS, TAPS))
            rolled = pltpu.roll(wide, 0, 1, stride=1, stride_axis=0)
            start = (j * STEP + sub + 1) * TAPS
            if not isinstance(j, int):
                start = pl.multiple_of(start, TAPS)
            blocks[slot, pl.ds(start, TAPS), :] = jnp.where(keep, rolled, prev).astype(BF16)
            prev = rolled
        return prev

    @pl.loop(0, MINE // 2)
    def _(c):
        near[c, pl.ds(0, TAPS), :] = jnp.zeros((TAPS, TAPS), BF16)
        late[c, pl.ds(0, TAPS), :] = jnp.zeros((TAPS, TAPS), BF16)
        lax.fori_loop(
            0, TBLK // STEP, lambda j, prev: build(near, c, c, j, prev), jnp.zeros((TAPS, TAPS), F32)
        )

    blank = jnp.zeros((ROWS, TAPS), F32)
    for half in range(2):
        shifted[0, half, pl.ds(0, ROWS), :] = blank
        shifted[1, half, pl.ds(ROWS, ROWS), :] = blank

    @pl.loop(0, CTX)
    def _(p):
        remote(send.at[p], recv.at[p], ss.at[p], sr.at[p], p, across).wait_recv()
        for half in range(2):
            part = recv[p, :, :, pl.ds(TAPS * half, TAPS)].astype(F32)
            start = pl.multiple_of(p * 4 * MINE, 4 * MINE)
            rows_in[half, pl.ds(start, 4 * MINE), :] = part.reshape(4 * MINE, TAPS)

    def channel(c, r, blocks, slot, ahead):
        for half in range(2):
            shifted[0, half, pl.ds(ROWS, ROWS), :] = rows_in[half, pl.ds(c, ROWS, stride=2 * MINE), :]
            shifted[1, half, pl.ds(0, ROWS), :] = rows_in[half, pl.ds(c + MINE, ROWS, stride=2 * MINE), :]
        for s in range(SEGS):
            n = ROWS - PER * s
            for e in range(PER):
                far = PER * s + e
                for part in range(2):
                    half = 1 - part
                    lanes = pl.ds(e * BLK + part * TAPS, TAPS)
                    lhs[s, pl.ds(0, n), lanes] = shifted[0, half, pl.ds(ROWS - e, n), :].astype(BF16)
                    lhs[s, pl.ds(n, n), lanes] = shifted[1, half, pl.ds(far, n), :].astype(BF16)
        prev = jnp.zeros((TAPS, TAPS), F32)
        for s in range(SEGS):
            n = ROWS - PER * s
            depth = PER * BLK
            if ahead:
                prev = build(late, slot, c + MINE // 2, s, prev)
            rhs = jnp.concatenate(
                [
                    blocks[slot, pl.ds(depth * s, depth), :],
                    blocks[slot, pl.ds(depth * s + TAPS, depth), :],
                ],
                axis=1,
            )
            out = jnp.dot(lhs[s, pl.ds(0, 2 * n), :], rhs, preferred_element_type=F32)
            if s == 0:
                acc[...] = out
            else:
                acc[pl.ds(PER * s, n), :] += out[:n]
                acc[pl.ds(ROWS, n), :] += out[n:]
        for half in range(2):
            lanes = pl.ds(TAPS * half, TAPS)
            rows_out[half, pl.ds(r, ROWS, stride=2 * PAIR), :] = acc[pl.ds(0, ROWS), lanes]
            rows_out[half, pl.ds(r + PAIR, ROWS, stride=2 * PAIR), :] = acc[pl.ds(ROWS, ROWS), lanes]

    def reply(group):
        for half in range(2):
            part = rows_out[half].reshape(CTX, 4 * PAIR, TAPS)
            back_send[group, :, :, pl.ds(TAPS * half, TAPS)] = part.astype(BF16)

        @pl.loop(0, CTX)
        def _(k):
            p = ctx_peer(k)
            remote(
                back_send.at[group, p], back.at[group, me],
                bs.at[group, p], br.at[group, me], p, across,
            ).start()

    @pl.loop(0, GROUPS // 2)
    def _(group):
        @pl.loop(0, PAIR)
        def _(r):
            c = group * PAIR + r
            channel(c, r, near, c, True)

        reply(group)

    @pl.loop(GROUPS // 2, GROUPS)
    def _(group):
        @pl.loop(0, PAIR)
        def _(r):
            c = group * PAIR + r
            channel(c, r, late, c - MINE // 2, False)

        reply(group)

    @pl.loop(1, CH)
    def _(k):
        p = ch_peer(k)
        remote(columns(p), taps_mid.at[p], fs1.at[p], fr1.at[p], me, p).wait_send()

    @pl.loop(0, CTX)
    def _(k):
        p = ctx_peer(k)
        remote(taps_send.at[p], taps_recv.at[p], fs2.at[p], fr2.at[p], p, across).wait_send()
        remote(send.at[p], recv.at[p], ss.at[p], sr.at[p], p, across).wait_send()

    @pl.loop(0, GROUPS)
    def _(group):
        @pl.loop(0, CTX)
        def _(k):
            p = ctx_peer(k)
            done = remote(
                back_send.at[group, p], back.at[group, p],
                bs.at[group, p], br.at[group, p], p, across,
            )
            done.wait_send()
            done.wait_recv()


def finish_kernel(query, key, value, grad, gain, back, output, query_grad, key_grad, value_grad, wide):
    unit = eye(BLK)
    mirror = eye(BLK, True)
    scale = gain[...]
    for part in range(2):
        lanes = pl.ds(TAPS * part, TAPS)
        wide[part] = back[:, :, :, lanes].astype(F32).reshape(GROUPS * CTX * 4 * PAIR, TAPS)

    def rows(first):
        columns = []
        for part in range(2):
            pieces = []
            for c in range(MINE):
                start = c // PAIR * (CTX * 4 * PAIR) + first + c % PAIR
                pieces.append(wide[part, pl.ds(start, CTX, stride=4 * PAIR), :])
            columns.append(jnp.concatenate(pieces, axis=0))
        return jnp.concatenate(columns, axis=1).astype(BF16)

    for half in range(2):
        toks = pl.ds(BLK * half, BLK)
        conv = rows(2 * PAIR * half)
        refl = rows(2 * PAIR * half + PAIR)
        q = query[toks, :].astype(F32)
        k = key[toks, :].astype(F32)
        v = value[toks, :].astype(F32)
        g = grad[toks, :].astype(F32)
        summed = times_transposed(unit, conv) + scale * (k * v).astype(BF16).astype(F32)
        output[toks, :] = (q * summed).astype(BF16)
        query_grad[toks, :] = (g * summed).astype(BF16)
        grad_sum = times_transposed(mirror, refl) + scale * (g * q).astype(BF16).astype(F32)
        key_grad[toks, :] = (grad_sum * v).astype(BF16)
        value_grad[toks, :] = (grad_sum * k).astype(BF16)


def shards(query, key, value, grad, taps, gain):
    vmem = pl.BlockSpec(memory_space=pltpu.VMEM)
    anywhere = pl.BlockSpec(memory_space=pl.ANY)
    dma = pltpu.SemaphoreType.DMA
    tile = (CTX, 2, 2 * MINE, BLK)
    reply = (GROUPS, CTX, 4 * PAIR, BLK)
    back = pl.pallas_call(
        convolve_kernel,
        out_shape=jax.ShapeDtypeStruct(reply, BF16),
        in_specs=[anywhere] * 5,
        out_specs=anywhere,
        scratch_shapes=[
            pltpu.VMEM(query.shape, BF16),
            pltpu.VMEM(query.shape, BF16),
            pltpu.VMEM(query.shape, BF16),
            pltpu.VMEM(query.shape, BF16),
            pltpu.VMEM((32, CH * 256), BF16),
            pltpu.VMEM((CH, 32, 256), BF16),
            pltpu.VMEM((CTX, MINE, 512), BF16),
            pltpu.VMEM((CTX, MINE, 512), BF16),
            pltpu.VMEM((TBLK, MINE, TAPS), F32),
            pltpu.VMEM(tile, BF16),
            pltpu.VMEM(tile, BF16),
            pltpu.VMEM((2, ROWS * 2 * MINE, TAPS), F32),
            pltpu.VMEM((2, ROWS * 2 * PAIR, TAPS), F32),
            pltpu.VMEM(reply, BF16),
            pltpu.VMEM((MINE // 2, (TBLK + 1) * TAPS, TAPS), BF16),
            pltpu.VMEM((MINE // 2, (TBLK + 1) * TAPS, TAPS), BF16),
            pltpu.VMEM((2, 2, 2 * ROWS, TAPS), F32),
            pltpu.VMEM((SEGS, 2 * ROWS, PER * BLK), BF16),
            pltpu.VMEM((2 * ROWS, BLK), F32),
            dma((1,)), dma((5,)),
            dma((CH,)), dma((CH,)),
            dma((CTX,)), dma((CTX,)),
            dma((CTX,)), dma((CTX,)),
            dma((GROUPS, CTX)), dma((GROUPS, CTX)),
        ],
        compiler_params=pltpu.CompilerParams(
            collective_id=0, has_side_effects=True, vmem_limit_bytes=60 * 2**20
        ),
        name="convolve",
    )(query, key, value, grad, taps.T)
    shape = jax.ShapeDtypeStruct(query.shape, BF16)
    return pl.pallas_call(
        finish_kernel,
        out_shape=(shape,) * 4,
        in_specs=[vmem] * 6,
        out_specs=(vmem,) * 4,
        scratch_shapes=[pltpu.VMEM((2, GROUPS * CTX * 4 * PAIR, TAPS), F32)],
        name="finish",
    )(query, key, value, grad, gain.reshape(1, -1), back)


def solution(mesh):
    placed = (
        P("ctx", "ch"),
        P("ctx", "ch"),
        P("ctx", "ch"),
        P("ctx", "ch"),
        P(None, ("ch", "ctx")),
        P("ch"),
    )
    return jax.shard_map(
        shards,
        mesh=mesh,
        in_specs=placed,
        out_specs=(P("ctx", "ch"), P("ctx", "ch"), P("ctx", "ch"), P("ctx", "ch")),
        check_vma=False,
    )
```
